32 devices in a mesh: seq: 8 (over z, x), mp: 4 (over y, core).
Axes of the slice: x: 2, y: 2, z: 4, core: 2. Of those that a mesh axis runs over, the one named last changes fastest.
Arguments:
- tokens: bfloat16 [32768, 1152], P(('seq', 'mp')), may hold values from -6 to 6
- cotangent: bfloat16 [32768, 1152], P(('seq', 'mp')), may hold values from -6 to 6
- segment: int32 [32768], P(('seq', 'mp')), may hold values from 0 to 3, as said below
- timestep: int32 [128], P(('seq', 'mp')), may hold values from 0 to 999
- head_mask: int32 [128, 16], P(('seq', 'mp')), may hold values 0 or 1
- chan_mask: int32 [128, 16], P(('seq', 'mp')), may hold values 0 or 1
- router_keep: int32 [32768], P(('seq', 'mp')), may hold values from 0 to 1, as said below
- ada_weight: bfloat16 [1152, 6912], P('mp'), may hold values from -0.1875 to 0.1875
- ada_bias: bfloat16 [6912], replicated, may hold values from -3 to 3
- qkv_weight: bfloat16 [1152, 3456], P('mp'), may hold values from -0.1875 to 0.1875
- qv_bias: bfloat16 [2304], replicated, may hold values from -2 to 2
- proj_weight: bfloat16 [1152, 1152], P('mp'), may hold values from -0.5 to 0.5
- proj_bias: bfloat16 [1152], replicated, may hold values from -2 to 2
- up_weight: bfloat16 [1152, 4608], P('mp'), may hold values from -0.1875 to 0.1875
- up_bias: bfloat16 [4608], replicated, may hold values from -2 to 2
- down_weight: bfloat16 [4608, 1152], P('mp'), may hold values from -0.09375 to 0.09375
- down_bias: bfloat16 [1152], replicated, may hold values from -2 to 2
Outputs:
- output: bfloat16 [32768, 1152], P(('seq', 'mp'))
- token_grad: float32 [32768, 1152], P(('seq', 'mp'))
- ada_weight_grad: float32 [1152, 6912], P('mp', 'seq')
- qkv_weight_grad: float32 [1152, 3456], P('mp', 'seq')
- proj_weight_grad: float32 [1152, 1152], P('mp', 'seq')
- up_weight_grad: float32 [1152, 4608], P('mp', 'seq')
- down_weight_grad: float32 [4608, 1152], P('mp', 'seq')
- ada_bias_grad: float32 [6912], replicated
- qv_bias_grad: float32 [2304], replicated
- proj_bias_grad: float32 [1152], replicated
- up_bias_grad: float32 [4608], replicated
- down_bias_grad: float32 [1152], replicated
The draws below stay inside these ranges and needn't reach their ends.
Inputs may be any that keep to these rules, and one draw needn't show every extreme that they name: The 1024 tokens of each device are one item (segment 0 throughout) or 4 items of 256 tokens with segments 0 to 3 in order; exactly half of the devices hold one item, and their unused item slots do not matter. `router_keep`: exactly 24576 entries are 1; how many of a device's tokens are kept differs from device to device.
All inputs are finite; a program needn't handle non-finite values. No bound on the sum of `head_mask` or of `chan_mask` on one device may be relied on, other than what follows from the above.
Results may differ from the reference program's by a relative error of at most 0.012.
Values may be sent and summed in bfloat16 or wider, within the bound.
No kernel may reach another device: no remote copies, remote signals or barrier semaphores. Data moves between devices by JAX's collectives and lax.ppermute only.
A program may use at most 320 MiB of HBM per device.

```python
import math
import jax
import jax.numpy as jnp
from jax import lax

D = 1152
H = 16
HD = 72
FF = 4608
CG = 16
TOK_DEV = 1024
SHORT = 256
KEEP_DEV = 768
SLOTS = 4
TOKENS = 32768
ITEMS = 128


def draw_segment(key, part):
    groups = TOKENS // TOK_DEV
    shuffled = jax.random.permutation(key, groups)
    single = (shuffled < groups // 2).astype(jnp.int32)[:, None]
    position = jnp.arange(TOK_DEV, dtype=jnp.int32)[None, :]
    return ((1 - single) * (position // SHORT)).reshape(TOKENS)


def draw_router_keep(key, part):
    groups = TOKENS // TOK_DEV
    device_key, token_key = jax.random.split(key)
    device_bias = jax.random.randint(device_key, (groups, 1), 0, 1024)
    token_score = jax.random.randint(token_key, (groups, TOK_DEV), 0, 1024)
    scores = ((device_bias + token_score) * TOKENS).reshape(TOKENS) + jnp.arange(TOKENS, dtype=jnp.int32)
    chosen = lax.top_k(scores, KEEP_DEV * groups)[1]
    return jnp.zeros((TOKENS,), jnp.int32).at[chosen].set(1)


def place_ends(values, own_key, smallest, top_value):
    extent = values.shape
    index_at = [jax.random.randint(jax.random.fold_in(own_key, axis), (), 0, extent[axis]) for axis in range(len(extent))]
    values = values.at[tuple(index_at)].set(smallest)
    longest = extent.index(max(extent))
    index_at[longest] = (index_at[longest] + 1) % extent[longest]
    return values.at[tuple(index_at)].set(top_value)


def levels(stream_key, extent, shards, smallest, top_value):
    def one(axis_at, parts):
        steps = jax.random.uniform(jax.random.fold_in(jax.random.fold_in(stream_key, 6), axis_at), (parts,), jnp.float32, smallest / len(shards), top_value / len(shards))
        return jnp.repeat(jnp.exp(steps), extent[axis_at] // parts).reshape((-1,) + (1,) * (len(extent) - axis_at - 1))

    level = one(*shards[0])
    for cut in shards[1:]:
        level = level * one(*cut)
    return level


def normal_values(rng, shape, width, most, cuts=(), held_as=jnp.bfloat16):
    values = jax.random.normal(rng, shape, jnp.float32) * width
    if len(cuts) > 0:
        values = levels(rng, shape, cuts, -0.22, 0.18) * values
    return jnp.clip(values, min=-most, max=most).astype(held_as)


def setup_inputs(seed: int = 0) -> dict:
    keys = jax.random.split(jax.random.key(seed), 18)
    return {
        "tokens": normal_values(keys[0], (TOKENS, D), 1.0, 6.0, ((0, 32),)),
        "cotangent": normal_values(keys[1], (TOKENS, D), 1.0, 6.0, ((0, 32),)),
        "segment": draw_segment(jax.random.fold_in(keys[17], 71), 0),
        "timestep": place_ends(jax.random.randint(keys[3], (ITEMS,), 0, 1000), jax.random.fold_in(keys[3], 1), 0, 999).astype(jnp.int32),
        "head_mask": place_ends((jax.random.randint(keys[4], (ITEMS, H), 0, 4) < 3).astype(jnp.int32), jax.random.fold_in(keys[4], 1), 0, 1),
        "chan_mask": place_ends((jax.random.randint(keys[5], (ITEMS, CG), 0, 4) < 3).astype(jnp.int32), jax.random.fold_in(keys[5], 1), 0, 1),
        "router_keep": draw_router_keep(jax.random.fold_in(keys[17], 71), 0),
        "ada_weight": normal_values(keys[7], (D, 6 * D), D ** -0.5, 0.1875, ((0, 4),)),
        "ada_bias": normal_values(keys[8], (6 * D,), 0.5, 3.0),
        "qkv_weight": normal_values(keys[9], (D, 3 * D), D ** -0.5, 0.1875, ((0, 4),)),
        "qv_bias": normal_values(keys[10], (2 * D,), 0.3, 2.0),
        "proj_weight": normal_values(keys[11], (D, D), (D // 8) ** -0.5, 0.5, ((0, 4),)),
        "proj_bias": normal_values(keys[12], (D,), 0.3, 2.0),
        "up_weight": normal_values(keys[13], (D, FF), D ** -0.5, 0.1875, ((0, 4),)),
        "up_bias": normal_values(keys[14], (FF,), 0.3, 2.0),
        "down_weight": normal_values(keys[15], (FF, D), FF ** -0.5, 0.09375, ((0, 4),)),
        "down_bias": normal_values(keys[16], (D,), 0.3, 2.0),
    }


@jax.custom_vjp
def low(v):
    return lax.optimization_barrier(v.astype(jnp.bfloat16)).astype(jnp.float32)

@jax.custom_vjp
def low_back(v):
    return v

def low_keep(v):
    return (low(v), None)

def low_pass(kept, grad):
    return (grad,)

def back_keep(v):
    return (v, None)

def back_low(kept, grad):
    return (low(grad),)
low.defvjp(low_keep, low_pass)
low_back.defvjp(back_keep, back_low)

def product(left_side, right_side):
    return jnp.dot(left_side, right_side, precision=lax.Precision.HIGHEST, preferred_element_type=jnp.float32)

def sinusoid(stamps):
    half_width = D // 2
    frequency = jnp.exp(-math.log(10000.0) * jnp.arange(half_width).astype(jnp.float32) / half_width)
    angles = stamps.astype(jnp.float32)[:, None] * frequency[None, :]
    return jnp.concatenate([jnp.cos(angles), jnp.sin(angles)], axis=1)

def normalize(values):
    center = values - lax.optimization_barrier(jnp.mean(values, axis=1, keepdims=True))
    return center * lax.rsqrt(lax.optimization_barrier(jnp.mean(center * center, axis=1, keepdims=True)) + 1e-06)

def split_heads(values):
    return values.reshape(TOK_DEV, H, HD).transpose(1, 0, 2)

def group_forward(params, tok_rows, seg_rows, stamps, head_keep, chan_keep, keep_rows):
    ada_weight, ada_bias, qkv_weight, qv_bias, proj_weight, proj_bias, up_weight, up_bias, down_weight, down_bias = params
    condition = low(jax.nn.silu(sinusoid(stamps)))
    modulation = product(condition, ada_weight) + ada_bias
    one_hot = (seg_rows[:, None] == jnp.arange(SLOTS)[None, :]).astype(jnp.float32)
    tok_mod = product(one_hot, modulation)
    first_shift, first_scale, first_gate, second_shift, second_scale, second_gate = [tok_mod[:, section * D:(section + 1) * D] for section in range(6)]
    normed = low(normalize(tok_rows) * (1.0 + first_scale) + first_shift)
    joined = product(normed, qkv_weight)
    queries = low(low_back(joined[:, :D] + qv_bias[:D]))
    keys_all = low(low_back(joined[:, D:2 * D]))
    values_all = low(low_back(joined[:, 2 * D:] + qv_bias[D:]))
    same_item = seg_rows[:, None] == seg_rows[None, :]

    def one_head(triple):
        head_queries, head_keys, head_values = triple
        scores = low_back(product(head_queries, head_keys.T) * HD ** (-0.5))
        scores = jnp.where(same_item, scores, -1e+30)
        attention = low(jax.nn.softmax(scores, axis=1))
        return product(attention, head_values)
    attended = lax.map(jax.checkpoint(one_head), (split_heads(queries), split_heads(keys_all), split_heads(values_all)))
    head_gate = product(one_hot, head_keep.astype(jnp.float32))
    attended = attended * head_gate.T[:, :, None]
    attn_cat = low(low_back(attended.transpose(1, 0, 2).reshape(TOK_DEV, D)))
    branch = low_back(product(attn_cat, proj_weight) + proj_bias)
    middle = tok_rows + first_gate * branch
    second_in = low(low_back(normalize(middle) * (1.0 + second_scale) + second_shift))
    pre_act = low_back(product(second_in, up_weight) + up_bias)
    chan_gate = product(one_hot, chan_keep.astype(jnp.float32))
    activated = jax.nn.gelu(pre_act, approximate=True).reshape(TOK_DEV, CG, FF // CG) * chan_gate[:, :, None]
    hidden = low(activated.reshape(TOK_DEV, FF))
    mlp_out = low(low_back(product(hidden, down_weight) + down_bias))
    return middle + keep_rows.astype(jnp.float32)[:, None] * second_gate * mlp_out

def reference(tokens, cotangent, segment, timestep, head_mask, chan_mask, router_keep, ada_weight, ada_bias, qkv_weight, qv_bias, proj_weight, proj_bias, up_weight, up_bias, down_weight, down_bias):
    params = tuple((weight.astype(jnp.float32) for weight in (ada_weight, ada_bias, qkv_weight, qv_bias, proj_weight, proj_bias, up_weight, up_bias, down_weight, down_bias)))
    groups = TOKENS // TOK_DEV
    grouped = (segment.reshape(groups, TOK_DEV), timestep.reshape(groups, SLOTS), head_mask.reshape(groups, SLOTS, H), chan_mask.reshape(groups, SLOTS, CG), router_keep.reshape(groups, TOK_DEV))

    def forward(params_in, tok_all):

        def one_group(pieces):
            tok_rows, seg_rows, stamps, head_keep, chan_keep, keep_rows = pieces
            return group_forward(params_in, tok_rows, seg_rows, stamps, head_keep, chan_keep, keep_rows)
        result = lax.map(jax.checkpoint(one_group), (tok_all.reshape(groups, TOK_DEV, D),) + grouped)
        return result.reshape(TOKENS, D)
    output, pullback = jax.vjp(forward, params, tokens.astype(jnp.float32))
    param_grads, token_grad = pullback(cotangent.astype(jnp.float32))
    return (output.astype(jnp.bfloat16), token_grad, param_grads[0], param_grads[2], param_grads[4], param_grads[6], param_grads[8], param_grads[1], param_grads[3], param_grads[5], param_grads[7], param_grads[9])
```

```python
import math

import jax
import jax.numpy as jnp
from jax import lax
from jax.sharding import PartitionSpec as P


HIGHEST = lax.Precision.HIGHEST
EVERY = ("seq", "mp")


def sinusoid(stamps, model_width):
    half_width = model_width // 2
    frequency = jnp.exp(
        -math.log(10000.0) * jnp.arange(half_width).astype(jnp.float32) / half_width
    )
    angles = stamps.astype(jnp.float32)[:, None] * frequency[None, :]
    return jnp.concatenate([jnp.cos(angles), jnp.sin(angles)], axis=1)


def norm_stats(values):
    center = values - jnp.mean(values, axis=-1, keepdims=True)
    inv = lax.rsqrt(jnp.mean(center * center, axis=-1, keepdims=True) + 1e-06)
    return center * inv, inv


def norm_back(kept, inv, normal):
    mean_kept = jnp.mean(kept, axis=-1, keepdims=True)
    mean_both = jnp.mean(kept * normal, axis=-1, keepdims=True)
    return inv * (kept - mean_kept - normal * mean_both)


def split_heads(values, head_count):
    row_count, model_width = values.shape
    return values.reshape(row_count, head_count, model_width // head_count).transpose(1, 0, 2)


def merge_heads(values):
    head_count, row_count, head_size = values.shape
    return values.transpose(1, 0, 2).reshape(row_count, head_count * head_size)


def masked_scores(head_queries, head_keys, same_item, score_scale):
    scores = (
        jnp.einsum("qe,ke->qk", head_queries, head_keys, preferred_element_type=jnp.float32)
        * score_scale
    )
    return jnp.where(same_item, scores, -1e30)


def attend_forward(triple, same_item, score_scale):
    head_queries, head_keys, head_values = triple
    scores = masked_scores(head_queries, head_keys, same_item, score_scale)
    row_max = jnp.max(scores, axis=1, keepdims=True)
    exp_scores = jnp.exp(scores - row_max)
    row_total = jnp.sum(exp_scores, axis=1, keepdims=True)
    attention = (exp_scores / row_total).astype(jnp.bfloat16)
    result = jnp.dot(attention, head_values, preferred_element_type=jnp.float32)
    return (result, (row_max + jnp.log(row_total))[:, 0])


def attend_backward(quintet, same_item, score_scale):
    head_queries, head_keys, head_values, head_grad, log_total = quintet
    scores = masked_scores(head_queries, head_keys, same_item, score_scale)
    probs_full = jnp.exp(scores - log_total[:, None])
    attention = probs_full.astype(jnp.bfloat16)
    grad_soft = jnp.einsum("qe,ke->qk", head_grad, head_values, preferred_element_type=jnp.float32)
    row_inner = jnp.sum(grad_soft * probs_full, axis=1, keepdims=True)
    grad_scores = (probs_full * (grad_soft - row_inner)).astype(jnp.bfloat16)
    grad_queries = jnp.dot(grad_scores, head_keys, preferred_element_type=jnp.float32) * score_scale
    grad_keys = (
        jnp.einsum("qk,qe->ke", grad_scores, head_queries, preferred_element_type=jnp.float32)
        * score_scale
    )
    grad_values = jnp.einsum("qk,qe->ke", attention, head_grad, preferred_element_type=jnp.float32)
    return (grad_queries, grad_keys, grad_values)


def swap(values, axis_name, bit):
    size = lax.axis_size(axis_name)
    return lax.ppermute(values, axis_name, [(i, i ^ bit) for i in range(size)])


def pick(values, dim, major, index):
    shape = values.shape
    inner = shape[dim] // (2 * major)
    cut = values.reshape(shape[:dim] + (major, 2, inner) + shape[dim + 1 :])
    cut = lax.dynamic_index_in_dim(cut, index, dim + 1, keepdims=False)
    return cut.reshape(shape[:dim] + (major * inner,) + shape[dim + 1 :])


def halve(values, dim, axis_name, level, bits):
    mine = (lax.axis_index(axis_name) >> level) & 1
    major = 2 ** bits.index(level)
    sent = pick(values, dim, major, 1 - mine).astype(jnp.bfloat16)
    came = swap(sent, axis_name, 1 << level)
    kept = pick(values, dim, major, mine)
    bits.remove(level)
    return kept.astype(jnp.float32) + came.astype(jnp.float32)


def levels_of(axis_name):
    return list(range(lax.axis_size(axis_name).bit_length() - 1))[::-1]


def grad_sum(split_side, whole_side, split_first):
    mp_bits = levels_of("mp")
    seq_bits = levels_of("seq")
    core = lax.axis_index("mp") & 1
    major = 2 ** mp_bits.index(0)

    def product(side):
        if split_first:
            return jnp.einsum("nd,ne->de", side, whole_side, preferred_element_type=jnp.float32)
        return jnp.einsum("ne,nd->ed", whole_side, side, preferred_element_type=jnp.float32)

    sent = product(pick(split_side, 1, major, 1 - core)).astype(jnp.bfloat16)
    came = swap(sent, "mp", 1)
    kept = product(pick(split_side, 1, major, core))
    total = kept + came.astype(jnp.float32)
    mp_bits.remove(0)
    mp_dim = 0 if split_first else 1
    for level in mp_bits[::-1]:
        total = halve(total.astype(jnp.bfloat16), mp_dim, "mp", level, mp_bits)
    order = [level for level in seq_bits[::-1] if level != 0] + [0]
    for level in order:
        total = halve(total.astype(jnp.bfloat16), 1 - mp_dim, "seq", level, seq_bits)
    return total if split_first else total.T


def gelu_parts(pre):
    inner = math.sqrt(2.0 / math.pi)
    square = pre * pre
    bend = jnp.tanh(inner * (pre + 0.044715 * pre * square))
    value = 0.5 * pre * (1.0 + bend)
    slope = 0.5 * (1.0 + bend) + 0.5 * pre * (1.0 - bend * bend) * inner * (
        1.0 + 3.0 * 0.044715 * square
    )
    return value, slope


def on_device(
    tokens,
    cotangent,
    segment,
    timestep,
    head_mask,
    chan_mask,
    router_keep,
    ada_weight,
    ada_bias,
    qkv_weight,
    qv_bias,
    proj_weight,
    proj_bias,
    up_weight,
    up_bias,
    down_weight,
    down_bias,
):
    row_count, model_width = tokens.shape
    slot_count = timestep.shape[0]
    head_count = head_mask.shape[1]
    group_count = chan_mask.shape[1]
    hidden_width = up_bias.shape[0]
    score_scale = (model_width // head_count) ** (-0.5)
    mp_size = lax.axis_size("mp")
    seq_size = lax.axis_size("seq")
    slot_rows = row_count // slot_count
    blocked = (slot_count, slot_rows, model_width)
    flat = (row_count, model_width)
    single = segment[row_count - 1] == 0

    row_width = model_width // mp_size
    first_col = lax.axis_index("mp") * row_width

    def condition_of(stamps):
        value = jax.nn.silu(sinusoid(stamps, model_width)).astype(jnp.bfloat16)
        return lax.dynamic_slice_in_dim(value, first_col, row_width, 1)

    stamp_float = timestep.astype(jnp.float32)
    peer_stamps = [stamp_float] + [swap(stamp_float, "mp", k) for k in range(1, mp_size)]
    group_cond = condition_of(jnp.concatenate(peer_stamps))
    group_mod = jnp.dot(group_cond, ada_weight, preferred_element_type=jnp.float32)
    group_mod = group_mod.reshape(mp_size, slot_count, 6 * model_width)
    modulation = group_mod[0] + ada_bias.astype(jnp.float32)
    for k in range(1, mp_size):
        modulation = modulation + swap(group_mod[k], "mp", k)

    full_qkv = lax.all_gather(qkv_weight, "mp", axis=0, tiled=True)
    full_proj = lax.all_gather(proj_weight, "mp", axis=0, tiled=True)
    full_up = lax.all_gather(up_weight, "mp", axis=0, tiled=True)
    full_down = lax.all_gather(down_weight, "mp", axis=0, tiled=True)

    slot_mod = jnp.where(single, modulation[:1], modulation)
    first_shift, first_scale, first_gate, second_shift, second_scale, second_gate = [
        slot_mod[:, None, section * model_width : (section + 1) * model_width]
        for section in range(6)
    ]
    head_gate = jnp.where(single, head_mask[:1], head_mask).astype(jnp.float32)
    head_rows = jnp.repeat(head_gate, slot_rows, axis=0)
    chan_gate = jnp.where(single, chan_mask[:1], chan_mask).astype(jnp.float32)
    unit_gate = jnp.repeat(chan_gate, hidden_width // group_count, axis=1)[:, None, :]
    keep_rows = router_keep.astype(jnp.float32).reshape(slot_count, slot_rows, 1)

    tok_float = tokens.astype(jnp.float32).reshape(blocked)
    first_normal, first_inv = norm_stats(tok_float)
    normed = (first_normal * (1.0 + first_scale) + first_shift).astype(jnp.bfloat16).reshape(flat)
    joined = jnp.dot(normed, full_qkv, preferred_element_type=jnp.float32)
    qv_float = qv_bias.astype(jnp.float32)
    queries = (joined[:, :model_width] + qv_float[:model_width]).astype(jnp.bfloat16)
    keys_all = joined[:, model_width : 2 * model_width].astype(jnp.bfloat16)
    values_all = (joined[:, 2 * model_width :] + qv_float[model_width:]).astype(jnp.bfloat16)
    same_item = segment[:, None] == segment[None, :]
    head_inputs = (
        split_heads(queries, head_count),
        split_heads(keys_all, head_count),
        split_heads(values_all, head_count),
    )
    attended, log_total = lax.map(
        lambda triple: attend_forward(triple, same_item, score_scale), head_inputs
    )
    attn_cat = merge_heads(attended * head_rows.T[:, :, None]).astype(jnp.bfloat16)
    branch = jnp.dot(attn_cat, full_proj, preferred_element_type=jnp.float32) + proj_bias.astype(
        jnp.float32
    )
    branch = branch.reshape(blocked)
    middle = tok_float + first_gate * branch
    second_normal, second_inv = norm_stats(middle)
    second_in = (second_normal * (1.0 + second_scale) + second_shift).astype(jnp.bfloat16)
    second_in = second_in.reshape(flat)

    pre_act = jnp.dot(second_in, full_up, preferred_element_type=jnp.float32) + up_bias.astype(
        jnp.float32
    )
    value, slope = gelu_parts(pre_act.reshape(slot_count, slot_rows, hidden_width))
    hidden = (value * unit_gate).astype(jnp.bfloat16).reshape(row_count, hidden_width)
    mlp_out = (
        jnp.dot(hidden, full_down, preferred_element_type=jnp.float32)
        + down_bias.astype(jnp.float32)
    ).astype(jnp.bfloat16)
    mlp_float = mlp_out.astype(jnp.float32).reshape(blocked)
    output = (middle + keep_rows * second_gate * mlp_float).astype(jnp.bfloat16).reshape(flat)

    grad_final = cotangent.astype(jnp.float32).reshape(blocked)
    grad_out = (keep_rows * second_gate * grad_final).astype(jnp.bfloat16).reshape(flat)
    grad_second_gate = jnp.sum(keep_rows * grad_final * mlp_float, axis=1)
    grad_hidden = jnp.einsum(
        "nd,fd->nf", grad_out, full_down, preferred_element_type=jnp.float32
    ).reshape(slot_count, slot_rows, hidden_width)
    grad_pre = (grad_hidden * unit_gate * slope).astype(jnp.bfloat16)
    grad_pre = grad_pre.reshape(row_count, hidden_width)
    down_piece = grad_sum(hidden, grad_out, False)
    grad_second = (
        jnp.einsum("nf,df->nd", grad_pre, full_up, preferred_element_type=jnp.float32)
        .astype(jnp.bfloat16)
        .astype(jnp.float32)
        .reshape(blocked)
    )
    up_piece = grad_sum(second_in, grad_pre, True)
    up_bias_grad = jnp.sum(grad_pre.astype(jnp.float32), axis=0)
    down_bias_grad = jnp.sum(grad_out.astype(jnp.float32), axis=0)

    grad_second_scale = jnp.sum(grad_second * second_normal, axis=1)
    grad_second_shift = jnp.sum(grad_second, axis=1)
    grad_middle = grad_final + norm_back(
        grad_second * (1.0 + second_scale), second_inv, second_normal
    )
    grad_branch = (first_gate * grad_middle).astype(jnp.bfloat16).reshape(flat)
    grad_first_gate = jnp.sum(grad_middle * branch, axis=1)
    grad_cat = jnp.einsum(
        "ne,de->nd", grad_branch, full_proj, preferred_element_type=jnp.float32
    ).astype(jnp.bfloat16)
    proj_piece = grad_sum(attn_cat, grad_branch, False)
    proj_bias_grad = jnp.sum(grad_branch.astype(jnp.float32), axis=0)

    lone = jnp.arange(slot_count)[:, None] == 0

    def per_item(sums):
        return jnp.where(single, jnp.where(lone, jnp.sum(sums, axis=0, keepdims=True), 0.0), sums)

    early = per_item(
        jnp.concatenate(
            [grad_first_gate, grad_second_shift, grad_second_scale, grad_second_gate], axis=1
        )
    )
    rest = jnp.zeros((early.shape[1] - 2 * model_width - slot_count,), jnp.float32)
    early_rows = jnp.concatenate(
        [
            early,
            up_bias_grad[None, :],
            jnp.concatenate([down_bias_grad, proj_bias_grad, stamp_float, rest])[None, :],
        ],
        axis=0,
    )
    all_early = lax.all_gather(early_rows, EVERY, axis=0, tiled=False)
    grad_heads = split_heads(grad_cat, head_count) * head_rows.T[:, :, None].astype(jnp.bfloat16)
    grad_queries, grad_keys, grad_values = lax.map(
        lambda quintet: attend_backward(quintet, same_item, score_scale),
        head_inputs + (grad_heads, log_total),
    )
    grad_joined = jnp.concatenate(
        [merge_heads(grad_queries), merge_heads(grad_keys), merge_heads(grad_values)], axis=1
    ).astype(jnp.bfloat16)
    grad_normed = jnp.einsum("ne,de->nd", grad_joined, full_qkv, preferred_element_type=jnp.float32)
    qkv_piece = grad_sum(normed, grad_joined, False)
    column_sums = jnp.sum(grad_joined.astype(jnp.float32), axis=0)
    qv_bias_grad = jnp.concatenate([column_sums[:model_width], column_sums[2 * model_width :]])
    grad_normed = grad_normed.reshape(blocked)
    token_grad = grad_middle + norm_back(
        grad_normed * (1.0 + first_scale), first_inv, first_normal
    )
    grad_first_scale = jnp.sum(grad_normed * first_normal, axis=1)
    grad_first_shift = jnp.sum(grad_normed, axis=1)
    late = per_item(jnp.concatenate([grad_first_shift, grad_first_scale], axis=1))
    late_rows = jnp.concatenate([late, qv_bias_grad[None, :]], axis=0)
    all_late = lax.all_gather(late_rows, EVERY, axis=0, tiled=False)

    item_count = slot_count * mp_size * seq_size
    all_modulation = jnp.concatenate(
        [all_late[:, :slot_count], all_early[:, :slot_count]], axis=2
    ).reshape(item_count, 6 * model_width)
    all_stamps = all_early[:, slot_count + 1, 2 * model_width : 2 * model_width + slot_count]
    cond_cols = condition_of(all_stamps.reshape(item_count)).astype(jnp.float32)
    col_width = 6 * model_width // seq_size
    mod_cols = lax.dynamic_slice_in_dim(
        all_modulation, lax.axis_index("seq") * col_width, col_width, 1
    )
    ada_piece = jnp.einsum("sd,sc->dc", cond_cols, mod_cols, precision=HIGHEST)
    ada_bias_grad = jnp.sum(all_modulation, axis=0)
    early_bias = jnp.sum(all_early[:, slot_count:], axis=0)
    return (
        output,
        token_grad.reshape(flat),
        ada_piece,
        qkv_piece,
        proj_piece,
        up_piece,
        down_piece.reshape(hidden_width // mp_size, model_width // seq_size),
        ada_bias_grad,
        jnp.sum(all_late[:, slot_count], axis=0),
        early_bias[1, model_width : 2 * model_width],
        early_bias[0],
        early_bias[1, :model_width],
    )


def solution(mesh):
    in_specs = (
        P(("seq", "mp"), None),
        P(("seq", "mp"), None),
        P(("seq", "mp")),
        P(("seq", "mp")),
        P(("seq", "mp"), None),
        P(("seq", "mp"), None),
        P(("seq", "mp")),
        P("mp", None),
        P(),
        P("mp", None),
        P(),
        P("mp", None),
        P(),
        P("mp", None),
        P(),
        P("mp", None),
        P(),
    )
    out_specs = (
        P(("seq", "mp"), None),
        P(("seq", "mp"), None),
        P("mp", "seq"),
        P("mp", "seq"),
        P("mp", "seq"),
        P("mp", "seq"),
        P("mp", "seq"),
        P(),
        P(),
        P(),
        P(),
        P(),
    )
    return jax.shard_map(
        on_device, mesh=mesh, in_specs=in_specs, out_specs=out_specs, check_vma=False
    )
```

```python
import math

import jax
import jax.numpy as jnp
from jax import lax
from jax.experimental import pallas as pl
from jax.experimental.pallas import tpu as pltpu
from jax.sharding import PartitionSpec as P


HIGHEST = lax.Precision.HIGHEST
EVERY = ("seq", "mp")
LANES = 128
WINDOW = 256
NT = (((1,), (1,)), ((), ()))


def sinusoid(stamps, model_width):
    half_width = model_width // 2
    frequency = jnp.exp(
        -math.log(10000.0) * jnp.arange(half_width).astype(jnp.float32) / half_width
    )
    angles = stamps.astype(jnp.float32)[:, None] * frequency[None, :]
    return jnp.concatenate([jnp.cos(angles), jnp.sin(angles)], axis=1)


def norm_stats(values):
    center = values - jnp.mean(values, axis=-1, keepdims=True)
    inv = lax.rsqrt(jnp.mean(center * center, axis=-1, keepdims=True) + 1e-06)
    return center * inv, inv


def norm_back(kept, inv, normal):
    mean_kept = jnp.mean(kept, axis=-1, keepdims=True)
    mean_both = jnp.mean(kept * normal, axis=-1, keepdims=True)
    return inv * (kept - mean_kept - normal * mean_both)


def head_window(head_size, width):
    first = pl.program_id(0) * head_size
    tile = jnp.minimum(first // LANES, width // LANES - WINDOW // LANES)
    start = first - tile * LANES
    lane = lax.broadcasted_iota(jnp.int32, (1, WINDOW), 1)
    inside = (lane >= start) & (lane < start + head_size)
    return pl.multiple_of(tile * LANES, LANES), inside


def dot32(left, right):
    return jnp.dot(left, right, preferred_element_type=jnp.float32)


def dot_nt(left, right):
    return lax.dot_general(left, right, NT, preferred_element_type=jnp.float32)


def attend_kernel(single_ref, gate_ref, q_ref, k_ref, v_ref, out_ref, log_ref, *, head_size, rows):
    count, width = q_ref.shape
    head = pl.program_id(0)
    base, inside = head_window(head_size, width)
    lanes = pl.ds(base, WINDOW)
    scale = head_size ** (-0.5)
    keys = k_ref[:, lanes] * inside.astype(jnp.bfloat16)
    values_t = v_ref[:, lanes].T

    def block(slot, first_key, key_count):
        mine = slice(slot * rows, (slot + 1) * rows)
        span = slice(first_key, first_key + key_count)
        scores = dot_nt(keys[span], q_ref[mine, lanes])
        peak = jnp.max(scores, axis=0, keepdims=True)
        weights = jnp.exp((scores - peak) * scale)
        total = jnp.sum(weights, axis=0, keepdims=True)
        summed = dot32(values_t[:, span], weights.astype(jnp.bfloat16))
        gate = gate_ref[slot, head].astype(jnp.float32)
        result = (summed * (gate / total)).T.astype(jnp.bfloat16)
        out_ref[mine, lanes] = jnp.where(inside, result, out_ref[mine, lanes])
        log_ref[0, :, mine] = peak * scale + jnp.log(total)

    @pl.when(single_ref[0] == 1)
    def _():
        for slot in range(count // rows):
            block(slot, 0, count)

    @pl.when(single_ref[0] == 0)
    def _():
        for slot in range(count // rows):
            block(slot, slot * rows, rows)


def attend_back_kernel(
    single_ref,
    gate_ref,
    q_ref,
    k_ref,
    v_ref,
    g_ref,
    log_ref,
    out_ref,
    key_sum,
    value_sum,
    *,
    head_size,
    rows,
):
    count, width = q_ref.shape
    head = pl.program_id(0)
    base, inside = head_window(head_size, width)
    lanes = pl.ds(base, WINDOW)
    scale = head_size ** (-0.5)
    only = inside.astype(jnp.bfloat16)
    keys = k_ref[:, lanes] * only
    keys_t = keys.T
    values = v_ref[:, lanes]

    def put(part, mine, result):
        there = pl.ds(pl.multiple_of(base + part * width, LANES), WINDOW)
        out_ref[mine, there] = jnp.where(
            inside, result.astype(jnp.bfloat16), out_ref[mine, there]
        )

    def block(slot, first_key, key_count):
        mine = slice(slot * rows, (slot + 1) * rows)
        span = slice(first_key, first_key + key_count)
        queries = q_ref[mine, lanes]
        gate = gate_ref[slot, head].astype(jnp.float32)
        grads = g_ref[mine, lanes] * (only.astype(jnp.float32) * gate).astype(jnp.bfloat16)
        scores = dot_nt(keys[span], queries)
        probs = jnp.exp(scores * scale - log_ref[0, :, mine])
        soft = dot_nt(values[span], grads)
        inner = jnp.sum(soft * probs, axis=0, keepdims=True)
        grad_scores = (probs * (soft - inner)).astype(jnp.bfloat16)
        put(0, mine, (dot32(keys_t[:, span], grad_scores) * scale).T)
        return dot32(grad_scores, queries), dot32(probs.astype(jnp.bfloat16), grads)

    @pl.when(single_ref[0] == 1)
    def _():
        for slot in range(count // rows):
            key_part, value_part = block(slot, 0, count)
            if slot == 0:
                key_sum[...] = key_part
                value_sum[...] = value_part
            else:
                key_sum[...] += key_part
                value_sum[...] += value_part
        put(1, slice(None), key_sum[...] * scale)
        put(2, slice(None), value_sum[...])

    @pl.when(single_ref[0] == 0)
    def _():
        for slot in range(count // rows):
            mine = slice(slot * rows, (slot + 1) * rows)
            key_part, value_part = block(slot, slot * rows, rows)
            put(1, mine, key_part * scale)
            put(2, mine, value_part)


def whole(shape):
    return pl.BlockSpec(shape, lambda n, *_: (0,) * len(shape))


def attend(single, gates, queries, keys, values):
    count, width = queries.shape
    heads = gates.shape[1]
    log_spec = pl.BlockSpec((1, 1, count), lambda n, *_: (n, 0, 0))
    return pl.pallas_call(
        lambda *refs: attend_kernel(
            *refs, head_size=width // heads, rows=count // gates.shape[0]
        ),
        grid_spec=pltpu.PrefetchScalarGridSpec(
            num_scalar_prefetch=2,
            grid=(heads,),
            in_specs=[whole((count, width))] * 3,
            out_specs=[whole((count, width)), log_spec],
        ),
        out_shape=[
            jax.ShapeDtypeStruct((count, width), jnp.bfloat16),
            jax.ShapeDtypeStruct((heads, 1, count), jnp.float32),
        ],
        name="attend",
    )(single, gates, queries, keys, values)


def attend_back(single, gates, queries, keys, values, grads, logs):
    count, width = queries.shape
    heads = gates.shape[1]
    log_spec = pl.BlockSpec((1, 1, count), lambda n, *_: (n, 0, 0))
    return pl.pallas_call(
        lambda *refs: attend_back_kernel(
            *refs, head_size=width // heads, rows=count // gates.shape[0]
        ),
        grid_spec=pltpu.PrefetchScalarGridSpec(
            num_scalar_prefetch=2,
            grid=(heads,),
            in_specs=[whole((count, width))] * 4 + [log_spec],
            out_specs=whole((count, 3 * width)),
            scratch_shapes=[pltpu.VMEM((count, WINDOW), jnp.float32)] * 2,
        ),
        out_shape=jax.ShapeDtypeStruct((count, 3 * width), jnp.bfloat16),
        name="attend_back",
    )(single, gates, queries, keys, values, grads, logs)


def swap(values, axis_name, bit):
    size = lax.axis_size(axis_name)
    return lax.ppermute(values, axis_name, [(i, i ^ bit) for i in range(size)])


def pick(values, dim, major, index):
    shape = values.shape
    inner = shape[dim] // (2 * major)
    cut = values.reshape(shape[:dim] + (major, 2, inner) + shape[dim + 1 :])
    cut = lax.dynamic_index_in_dim(cut, index, dim + 1, keepdims=False)
    return cut.reshape(shape[:dim] + (major * inner,) + shape[dim + 1 :])


def halve(values, dim, axis_name, level, bits):
    mine = (lax.axis_index(axis_name) >> level) & 1
    major = 2 ** bits.index(level)
    sent = pick(values, dim, major, 1 - mine).astype(jnp.bfloat16)
    came = swap(sent, axis_name, 1 << level)
    kept = pick(values, dim, major, mine)
    bits.remove(level)
    return kept.astype(jnp.float32) + came.astype(jnp.float32)


def levels_of(axis_name):
    return list(range(lax.axis_size(axis_name).bit_length() - 1))[::-1]


def grad_sum(split_side, whole_side, split_first):
    mp_bits = levels_of("mp")
    seq_bits = levels_of("seq")
    core = lax.axis_index("mp") & 1
    major = 2 ** mp_bits.index(0)

    def product(side):
        if split_first:
            return jnp.einsum("nd,ne->de", side, whole_side, preferred_element_type=jnp.float32)
        return jnp.einsum("ne,nd->ed", whole_side, side, preferred_element_type=jnp.float32)

    sent = product(pick(split_side, 1, major, 1 - core)).astype(jnp.bfloat16)
    came = swap(sent, "mp", 1)
    kept = product(pick(split_side, 1, major, core))
    total = kept + came.astype(jnp.float32)
    mp_bits.remove(0)
    mp_dim = 0 if split_first else 1
    for level in mp_bits[::-1]:
        total = halve(total.astype(jnp.bfloat16), mp_dim, "mp", level, mp_bits)
    order = [level for level in seq_bits[::-1] if level != 0] + [0]
    for level in order:
        total = halve(total.astype(jnp.bfloat16), 1 - mp_dim, "seq", level, seq_bits)
    return total if split_first else total.T


def gelu_parts(pre):
    inner = math.sqrt(2.0 / math.pi)
    square = pre * pre
    bend = jnp.tanh(inner * (pre + 0.044715 * pre * square))
    value = 0.5 * pre * (1.0 + bend)
    slope = 0.5 * (1.0 + bend) + 0.5 * pre * (1.0 - bend * bend) * inner * (
        1.0 + 3.0 * 0.044715 * square
    )
    return value, slope


def on_device(
    tokens,
    cotangent,
    segment,
    timestep,
    head_mask,
    chan_mask,
    router_keep,
    ada_weight,
    ada_bias,
    qkv_weight,
    qv_bias,
    proj_weight,
    proj_bias,
    up_weight,
    up_bias,
    down_weight,
    down_bias,
):
    row_count, model_width = tokens.shape
    slot_count = timestep.shape[0]
    group_count = chan_mask.shape[1]
    hidden_width = up_bias.shape[0]
    mp_size = lax.axis_size("mp")
    seq_size = lax.axis_size("seq")
    slot_rows = row_count // slot_count
    blocked = (slot_count, slot_rows, model_width)
    flat = (row_count, model_width)
    single = segment[row_count - 1] == 0

    row_width = model_width // mp_size
    first_col = lax.axis_index("mp") * row_width

    def condition_of(stamps):
        value = jax.nn.silu(sinusoid(stamps, model_width)).astype(jnp.bfloat16)
        return lax.dynamic_slice_in_dim(value, first_col, row_width, 1)

    stamp_float = timestep.astype(jnp.float32)
    peer_stamps = [stamp_float] + [swap(stamp_float, "mp", k) for k in range(1, mp_size)]
    group_cond = condition_of(jnp.concatenate(peer_stamps))
    group_mod = jnp.dot(group_cond, ada_weight, preferred_element_type=jnp.float32)
    group_mod = group_mod.reshape(mp_size, slot_count, 6 * model_width)
    modulation = group_mod[0] + ada_bias.astype(jnp.float32)
    for k in range(1, mp_size):
        modulation = modulation + swap(group_mod[k], "mp", k)

    full_qkv = lax.all_gather(qkv_weight, "mp", axis=0, tiled=True)
    full_proj = lax.all_gather(proj_weight, "mp", axis=0, tiled=True)
    full_up = lax.all_gather(up_weight, "mp", axis=0, tiled=True)
    full_down = lax.all_gather(down_weight, "mp", axis=0, tiled=True)

    slot_mod = jnp.where(single, modulation[:1], modulation)
    first_shift, first_scale, first_gate, second_shift, second_scale, second_gate = [
        slot_mod[:, None, section * model_width : (section + 1) * model_width]
        for section in range(6)
    ]
    chan_gate = jnp.where(single, chan_mask[:1], chan_mask).astype(jnp.float32)
    unit_gate = jnp.repeat(chan_gate, hidden_width // group_count, axis=1)[:, None, :]
    keep_rows = router_keep.astype(jnp.float32).reshape(slot_count, slot_rows, 1)

    tok_float = tokens.astype(jnp.float32).reshape(blocked)
    first_normal, first_inv = norm_stats(tok_float)
    normed = (first_normal * (1.0 + first_scale) + first_shift).astype(jnp.bfloat16).reshape(flat)
    joined = jnp.dot(normed, full_qkv, preferred_element_type=jnp.float32)
    qv_float = qv_bias.astype(jnp.float32)
    queries = (joined[:, :model_width] + qv_float[:model_width]).astype(jnp.bfloat16)
    keys_all = joined[:, model_width : 2 * model_width].astype(jnp.bfloat16)
    values_all = (joined[:, 2 * model_width :] + qv_float[model_width:]).astype(jnp.bfloat16)
    lone_flag = single.astype(jnp.int32).reshape(1)
    gates = jnp.where(single, head_mask[:1], head_mask)
    attn_cat, log_total = attend(lone_flag, gates, queries, keys_all, values_all)
    branch = jnp.dot(attn_cat, full_proj, preferred_element_type=jnp.float32) + proj_bias.astype(
        jnp.float32
    )
    branch = branch.reshape(blocked)
    middle = tok_float + first_gate * branch
    second_normal, second_inv = norm_stats(middle)
    second_in = (second_normal * (1.0 + second_scale) + second_shift).astype(jnp.bfloat16)
    second_in = second_in.reshape(flat)

    pre_act = jnp.dot(second_in, full_up, preferred_element_type=jnp.float32) + up_bias.astype(
        jnp.float32
    )
    value, slope = gelu_parts(pre_act.reshape(slot_count, slot_rows, hidden_width))
    hidden = (value * unit_gate).astype(jnp.bfloat16).reshape(row_count, hidden_width)
    mlp_out = (
        jnp.dot(hidden, full_down, preferred_element_type=jnp.float32)
        + down_bias.astype(jnp.float32)
    ).astype(jnp.bfloat16)
    mlp_float = mlp_out.astype(jnp.float32).reshape(blocked)
    output = (middle + keep_rows * second_gate * mlp_float).astype(jnp.bfloat16).reshape(flat)

    grad_final = cotangent.astype(jnp.float32).reshape(blocked)
    grad_out = (keep_rows * second_gate * grad_final).astype(jnp.bfloat16).reshape(flat)
    grad_second_gate = jnp.sum(keep_rows * grad_final * mlp_float, axis=1)
    grad_hidden = jnp.einsum(
        "nd,fd->nf", grad_out, full_down, preferred_element_type=jnp.float32
    ).reshape(slot_count, slot_rows, hidden_width)
    grad_pre = (grad_hidden * unit_gate * slope).astype(jnp.bfloat16)
    grad_pre = grad_pre.reshape(row_count, hidden_width)
    down_piece = grad_sum(hidden, grad_out, False)
    grad_second = (
        jnp.einsum("nf,df->nd", grad_pre, full_up, preferred_element_type=jnp.float32)
        .astype(jnp.bfloat16)
        .astype(jnp.float32)
        .reshape(blocked)
    )
    up_piece = grad_sum(second_in, grad_pre, True)
    up_bias_grad = jnp.sum(grad_pre.astype(jnp.float32), axis=0)
    down_bias_grad = jnp.sum(grad_out.astype(jnp.float32), axis=0)

    grad_second_scale = jnp.sum(grad_second * second_normal, axis=1)
    grad_second_shift = jnp.sum(grad_second, axis=1)
    grad_middle = grad_final + norm_back(
        grad_second * (1.0 + second_scale), second_inv, second_normal
    )
    grad_branch = (first_gate * grad_middle).astype(jnp.bfloat16).reshape(flat)
    grad_first_gate = jnp.sum(grad_middle * branch, axis=1)
    grad_cat = jnp.einsum(
        "ne,de->nd", grad_branch, full_proj, preferred_element_type=jnp.float32
    ).astype(jnp.bfloat16)
    proj_piece = grad_sum(attn_cat, grad_branch, False)
    proj_bias_grad = jnp.sum(grad_branch.astype(jnp.float32), axis=0)

    lone = jnp.arange(slot_count)[:, None] == 0

    def per_item(sums):
        return jnp.where(single, jnp.where(lone, jnp.sum(sums, axis=0, keepdims=True), 0.0), sums)

    early = per_item(
        jnp.concatenate(
            [grad_first_gate, grad_second_shift, grad_second_scale, grad_second_gate], axis=1
        )
    )
    rest = jnp.zeros((early.shape[1] - 2 * model_width - slot_count,), jnp.float32)
    early_rows = jnp.concatenate(
        [
            early,
            up_bias_grad[None, :],
            jnp.concatenate([down_bias_grad, proj_bias_grad, stamp_float, rest])[None, :],
        ],
        axis=0,
    )
    all_early = lax.all_gather(early_rows, EVERY, axis=0, tiled=False)
    grad_joined = attend_back(
        lone_flag, gates, queries, keys_all, values_all, grad_cat, log_total
    )
    grad_normed = jnp.einsum("ne,de->nd", grad_joined, full_qkv, preferred_element_type=jnp.float32)
    qkv_piece = grad_sum(normed, grad_joined, False)
    column_sums = jnp.sum(grad_joined.astype(jnp.float32), axis=0)
    qv_bias_grad = jnp.concatenate([column_sums[:model_width], column_sums[2 * model_width :]])
    grad_normed = grad_normed.reshape(blocked)
    token_grad = grad_middle + norm_back(
        grad_normed * (1.0 + first_scale), first_inv, first_normal
    )
    grad_first_scale = jnp.sum(grad_normed * first_normal, axis=1)
    grad_first_shift = jnp.sum(grad_normed, axis=1)
    late = per_item(jnp.concatenate([grad_first_shift, grad_first_scale], axis=1))
    late_rows = jnp.concatenate([late, qv_bias_grad[None, :]], axis=0)
    all_late = lax.all_gather(late_rows, EVERY, axis=0, tiled=False)

    item_count = slot_count * mp_size * seq_size
    all_modulation = jnp.concatenate(
        [all_late[:, :slot_count], all_early[:, :slot_count]], axis=2
    ).reshape(item_count, 6 * model_width)
    all_stamps = all_early[:, slot_count + 1, 2 * model_width : 2 * model_width + slot_count]
    cond_cols = condition_of(all_stamps.reshape(item_count)).astype(jnp.float32)
    col_width = 6 * model_width // seq_size
    mod_cols = lax.dynamic_slice_in_dim(
        all_modulation, lax.axis_index("seq") * col_width, col_width, 1
    )
    ada_piece = jnp.einsum("sd,sc->dc", cond_cols, mod_cols, precision=HIGHEST)
    ada_bias_grad = jnp.sum(all_modulation, axis=0)
    early_bias = jnp.sum(all_early[:, slot_count:], axis=0)
    return (
        output,
        token_grad.reshape(flat),
        ada_piece,
        qkv_piece,
        proj_piece,
        up_piece,
        down_piece.reshape(hidden_width // mp_size, model_width // seq_size),
        ada_bias_grad,
        jnp.sum(all_late[:, slot_count], axis=0),
        early_bias[1, model_width : 2 * model_width],
        early_bias[0],
        early_bias[1, :model_width],
    )


def solution(mesh):
    in_specs = (
        P(("seq", "mp"), None),
        P(("seq", "mp"), None),
        P(("seq", "mp")),
        P(("seq", "mp")),
        P(("seq", "mp"), None),
        P(("seq", "mp"), None),
        P(("seq", "mp")),
        P("mp", None),
        P(),
        P("mp", None),
        P(),
        P("mp", None),
        P(),
        P("mp", None),
        P(),
        P("mp", None),
        P(),
    )
    out_specs = (
        P(("seq", "mp"), None),
        P(("seq", "mp"), None),
        P("mp", "seq"),
        P("mp", "seq"),
        P("mp", "seq"),
        P("mp", "seq"),
        P("mp", "seq"),
        P(),
        P(),
        P(),
        P(),
        P(),
    )
    return jax.shard_map(
        on_device, mesh=mesh, in_specs=in_specs, out_specs=out_specs, check_vma=False
    )
```

```python
import math

import jax
import jax.numpy as jnp
from jax import lax
from jax.experimental import pallas as pl
from jax.experimental.pallas import tpu as pltpu
from jax.sharding import PartitionSpec as P


HIGHEST = lax.Precision.HIGHEST
LANES = 128
WINDOW = 256
NT = (((1,), (1,)), ((), ()))


def sinusoid(stamps, model_width):
    half_width = model_width // 2
    frequency = jnp.exp(
        -math.log(10000.0) * jnp.arange(half_width).astype(jnp.float32) / half_width
    )
    angles = stamps.astype(jnp.float32)[:, None] * frequency[None, :]
    return jnp.concatenate([jnp.cos(angles), jnp.sin(angles)], axis=1)


def norm_stats(values):
    center = values - jnp.mean(values, axis=-1, keepdims=True)
    inv = lax.rsqrt(jnp.mean(center * center, axis=-1, keepdims=True) + 1e-06)
    return center * inv, inv


def norm_back(kept, inv, normal):
    mean_kept = jnp.mean(kept, axis=-1, keepdims=True)
    mean_both = jnp.mean(kept * normal, axis=-1, keepdims=True)
    return inv * (kept - mean_kept - normal * mean_both)


def head_window(head_size, width, first_head=0):
    first = (pl.program_id(0) + first_head) * head_size
    tile = jnp.minimum(first // LANES, width // LANES - WINDOW // LANES)
    start = first - tile * LANES
    lane = lax.broadcasted_iota(jnp.int32, (1, WINDOW), 1)
    inside = (lane >= start) & (lane < start + head_size)
    return pl.multiple_of(tile * LANES, LANES), inside


def dot32(left, right):
    return jnp.dot(left, right, preferred_element_type=jnp.float32)


def dot_nt(left, right):
    return lax.dot_general(left, right, NT, preferred_element_type=jnp.float32)


def attend_kernel(single_ref, gate_ref, q_ref, k_ref, v_ref, out_ref, log_ref, *, head_size, rows):
    count, width = q_ref.shape
    head = pl.program_id(0)
    base, inside = head_window(head_size, width)
    lanes = pl.ds(base, WINDOW)
    scale = head_size ** (-0.5)
    keys = k_ref[:, lanes] * inside.astype(jnp.bfloat16)
    values_t = v_ref[:, lanes].T

    def block(slot, first_key, key_count):
        mine = slice(slot * rows, (slot + 1) * rows)
        span = slice(first_key, first_key + key_count)
        scores = dot_nt(keys[span], q_ref[mine, lanes])
        peak = jnp.max(scores, axis=0, keepdims=True)
        weights = jnp.exp((scores - peak) * scale)
        total = jnp.sum(weights, axis=0, keepdims=True)
        summed = dot32(values_t[:, span], weights.astype(jnp.bfloat16))
        gate = gate_ref[slot, head].astype(jnp.float32)
        result = (summed * (gate / total)).T.astype(jnp.bfloat16)
        out_ref[mine, lanes] = jnp.where(inside, result, out_ref[mine, lanes])
        log_ref[0, :, mine] = peak * scale + jnp.log(total)

    @pl.when(single_ref[0] == 1)
    def _():
        for slot in range(count // rows):
            block(slot, 0, count)

    @pl.when(single_ref[0] == 0)
    def _():
        for slot in range(count // rows):
            block(slot, slot * rows, rows)


def attend_back_kernel(
    single_ref,
    gate_ref,
    q_ref,
    k_ref,
    v_ref,
    g_ref,
    log_ref,
    *refs,
    head_size,
    rows,
    first_head,
    first_tile,
    end_tile,
):
    out_ref, key_sum, value_sum = refs[-3:]
    count, _ = q_ref.shape
    span_width = out_ref.shape[1] // 3
    head = pl.program_id(0) + first_head
    base, inside = head_window(head_size, end_tile * LANES, first_head)
    lanes = pl.ds(base, WINDOW)
    scale = head_size ** (-0.5)
    only = inside.astype(jnp.bfloat16)
    keys = k_ref[:, lanes] * only
    keys_t = keys.T
    values = v_ref[:, lanes]
    if len(refs) == 4:
        before = refs[0]
        before_width = before.shape[1] // 3

        @pl.when(pl.program_id(0) == 0)
        def _():
            for part in range(3):
                last = (part + 1) * before_width
                start = part * span_width
                out_ref[:, start : start + LANES] = before[:, last - LANES : last]

    def put(part, mine, result):
        there = base - first_tile * LANES + part * span_width
        there = pl.ds(pl.multiple_of(there, LANES), WINDOW)
        out_ref[mine, there] = jnp.where(
            inside, result.astype(jnp.bfloat16), out_ref[mine, there]
        )

    def block(slot, first_key, key_count):
        mine = slice(slot * rows, (slot + 1) * rows)
        span = slice(first_key, first_key + key_count)
        queries = q_ref[mine, lanes]
        gate = gate_ref[slot, head].astype(jnp.float32)
        grads = g_ref[mine, lanes] * (only.astype(jnp.float32) * gate).astype(jnp.bfloat16)
        scores = dot_nt(keys[span], queries)
        probs = jnp.exp(scores * scale - log_ref[0, :, mine])
        soft = dot_nt(values[span], grads)
        inner = jnp.sum(soft * probs, axis=0, keepdims=True)
        grad_scores = (probs * (soft - inner)).astype(jnp.bfloat16)
        put(0, mine, (dot32(keys_t[:, span], grad_scores) * scale).T)
        return dot32(grad_scores, queries), dot32(probs.astype(jnp.bfloat16), grads)

    @pl.when(single_ref[0] == 1)
    def _():
        for slot in range(count // rows):
            key_part, value_part = block(slot, 0, count)
            if slot == 0:
                key_sum[...] = key_part
                value_sum[...] = value_part
            else:
                key_sum[...] += key_part
                value_sum[...] += value_part
        put(1, slice(None), key_sum[...] * scale)
        put(2, slice(None), value_sum[...])

    @pl.when(single_ref[0] == 0)
    def _():
        for slot in range(count // rows):
            mine = slice(slot * rows, (slot + 1) * rows)
            key_part, value_part = block(slot, slot * rows, rows)
            put(1, mine, key_part * scale)
            put(2, mine, value_part)


def whole(shape):
    return pl.BlockSpec(shape, lambda n, *_: (0,) * len(shape))


def attend_cost(heads, count, head_size, products):
    return pl.CostEstimate(
        flops=2 * products * heads * count * count * WINDOW,
        transcendentals=heads * count * count,
        bytes_accessed=2 * (products + 2) * heads * count * head_size,
    )


def attend(single, gates, queries, keys, values):
    count, width = queries.shape
    heads = gates.shape[1]
    log_spec = pl.BlockSpec((1, 1, count), lambda n, *_: (n, 0, 0))
    return pl.pallas_call(
        lambda *refs: attend_kernel(
            *refs, head_size=width // heads, rows=count // gates.shape[0]
        ),
        grid_spec=pltpu.PrefetchScalarGridSpec(
            num_scalar_prefetch=2,
            grid=(heads,),
            in_specs=[whole((count, width))] * 3,
            out_specs=[whole((count, width)), log_spec],
        ),
        out_shape=[
            jax.ShapeDtypeStruct((count, width), jnp.bfloat16),
            jax.ShapeDtypeStruct((heads, 1, count), jnp.float32),
        ],
        name="attend",
        cost_estimate=attend_cost(heads, count, width // heads, 2),
    )(single, gates, queries, keys, values)


def attend_back(single, gates, queries, keys, values, grads, logs, group, groups, before=None):
    count, width = queries.shape
    heads = gates.shape[1]
    head_size = width // heads
    group_heads = heads // groups
    first_head = group * group_heads
    first_tile = first_head * head_size // LANES
    end_tile = -(-(first_head + group_heads) * head_size // LANES)
    log_spec = pl.BlockSpec((1, 1, count), lambda n, *_: (n + first_head, 0, 0))
    extra = [] if before is None else [before]
    out_width = 3 * (end_tile - first_tile) * LANES
    return pl.pallas_call(
        lambda *refs: attend_back_kernel(
            *refs,
            head_size=head_size,
            rows=count // gates.shape[0],
            first_head=first_head,
            first_tile=first_tile,
            end_tile=end_tile,
        ),
        grid_spec=pltpu.PrefetchScalarGridSpec(
            num_scalar_prefetch=2,
            grid=(group_heads,),
            in_specs=[whole((count, width))] * 4 + [log_spec] + [whole(x.shape) for x in extra],
            out_specs=whole((count, out_width)),
            scratch_shapes=[pltpu.VMEM((count, WINDOW), jnp.float32)] * 2,
        ),
        out_shape=jax.ShapeDtypeStruct((count, out_width), jnp.bfloat16),
        name="attend_back",
        cost_estimate=attend_cost(group_heads, count, head_size, 5),
    )(single, gates, queries, keys, values, grads, logs, *extra)


def swap(values, axis_name, bit):
    size = lax.axis_size(axis_name)
    return lax.ppermute(values, axis_name, [(i, i ^ bit) for i in range(size)])


def pick(values, dim, runs, index):
    inner = values.shape[dim] // (2 * runs)
    halves = [
        [lax.slice_in_dim(values, (2 * r + h) * inner, (2 * r + h + 1) * inner, axis=dim) for h in (0, 1)]
        for r in range(runs)
    ]
    chosen = [jnp.where(index == 1, high, low) for low, high in halves]
    return chosen[0] if runs == 1 else jnp.concatenate(chosen, axis=dim)


def levels_of(axis_name):
    return list(range(lax.axis_size(axis_name).bit_length() - 1))[::-1]


def sum_plan():
    steps = []
    mp_bits = levels_of("mp")
    for level in mp_bits[::-1]:
        steps.append((0, "mp", level, 2 ** mp_bits.index(level)))
        mp_bits = [bit for bit in mp_bits if bit != level]
    seq_bits = levels_of("seq")
    for level in seq_bits[:-1][::-1] + [0]:
        steps.append((1, "seq", level, 2 ** seq_bits.index(level)))
        seq_bits = [bit for bit in seq_bits if bit != level]
    return steps


def column_plan():
    levels = levels_of("seq")
    return [(1, "seq", level, 2 ** levels.index(level)) for level in levels[::-1]]


def my_bit(step):
    return (lax.axis_index(step[1]) >> step[2]) & 1


def ready(values, step):
    return values, pick(values, step[0], step[3], 1 - my_bit(step))


def launch(prepared, step):
    values, sent = prepared
    return values, swap(sent, step[1], 1 << step[2])


def settle(pending, step, kind=jnp.bfloat16):
    values, came = pending
    kept = pick(values, step[0], step[3], my_bit(step))
    return (kept.astype(jnp.float32) + came.astype(jnp.float32)).astype(kind)


def finish(pending, plan):
    for step, later in zip(plan[:-1], plan[1:]):
        pending = launch(ready(settle(pending, step), later), later)
    return settle(pending, plan[-1], jnp.float32)


def tie(*groups):
    return lax.optimization_barrier(groups)


def grad_product(rows_side, cols_side):
    product = jnp.einsum("nd,ne->de", rows_side, cols_side, preferred_element_type=jnp.float32)
    return product.astype(jnp.bfloat16)


def double_all(values, combine, steps):
    for step in steps:
        values = combine(values, swap(values, step[1], 1 << step[2]))
    return values


def join(mine, other):
    return jnp.concatenate([mine, other], axis=0)


def gelu_parts(pre):
    inner = math.sqrt(2.0 / math.pi)
    square = pre * pre
    bend = jnp.tanh(inner * (pre + 0.044715 * pre * square))
    value = 0.5 * pre * (1.0 + bend)
    slope = 0.5 * (1.0 + bend) + 0.5 * pre * (1.0 - bend * bend) * inner * (
        1.0 + 3.0 * 0.044715 * square
    )
    return value, slope


def on_device(
    tokens,
    cotangent,
    segment,
    timestep,
    head_mask,
    chan_mask,
    router_keep,
    ada_weight,
    ada_bias,
    qkv_weight,
    qv_bias,
    proj_weight,
    proj_bias,
    up_weight,
    up_bias,
    down_weight,
    down_bias,
):
    row_count, model_width = tokens.shape
    slot_count = timestep.shape[0]
    group_count = chan_mask.shape[1]
    hidden_width = up_bias.shape[0]
    mp_size = lax.axis_size("mp")
    slot_rows = row_count // slot_count
    blocked = (slot_count, slot_rows, model_width)
    flat = (row_count, model_width)
    single = segment[row_count - 1] == 0

    row_width = model_width // mp_size
    first_col = lax.axis_index("mp") * row_width

    def condition_of(stamps):
        value = jax.nn.silu(sinusoid(stamps, model_width)).astype(jnp.bfloat16)
        return lax.dynamic_slice_in_dim(value, first_col, row_width, 1)

    stamp_float = timestep.astype(jnp.float32)
    peer_stamps = [stamp_float] + [swap(stamp_float, "mp", k) for k in range(1, mp_size)]
    group_cond = condition_of(jnp.concatenate(peer_stamps))
    group_mod = jnp.dot(group_cond, ada_weight, preferred_element_type=jnp.float32)
    group_mod = group_mod.reshape(mp_size, slot_count, 6 * model_width)
    modulation = group_mod[0] + ada_bias.astype(jnp.float32)
    for k in range(1, mp_size):
        modulation = modulation + swap(group_mod[k], "mp", k)

    full_qkv = lax.all_gather(qkv_weight, "mp", axis=0, tiled=True)
    full_proj = lax.all_gather(proj_weight, "mp", axis=0, tiled=True)
    full_up = lax.all_gather(up_weight, "mp", axis=0, tiled=True)
    full_down = lax.all_gather(down_weight, "mp", axis=0, tiled=True)

    slot_mod = jnp.where(single, modulation[:1], modulation)
    first_shift, first_scale, first_gate, second_shift, second_scale, second_gate = [
        slot_mod[:, None, section * model_width : (section + 1) * model_width]
        for section in range(6)
    ]
    chan_gate = jnp.where(single, chan_mask[:1], chan_mask).astype(jnp.float32)
    unit_gate = jnp.repeat(chan_gate, hidden_width // group_count, axis=1)[:, None, :]
    keep_rows = router_keep.astype(jnp.float32).reshape(slot_count, slot_rows, 1)

    tok_float = tokens.astype(jnp.float32).reshape(blocked)
    first_normal, first_inv = norm_stats(tok_float)
    normed = (first_normal * (1.0 + first_scale) + first_shift).astype(jnp.bfloat16).reshape(flat)
    joined = jnp.dot(normed, full_qkv, preferred_element_type=jnp.float32)
    qv_float = qv_bias.astype(jnp.float32)
    queries = (joined[:, :model_width] + qv_float[:model_width]).astype(jnp.bfloat16)
    keys_all = joined[:, model_width : 2 * model_width].astype(jnp.bfloat16)
    values_all = (joined[:, 2 * model_width :] + qv_float[model_width:]).astype(jnp.bfloat16)
    lone_flag = single.astype(jnp.int32).reshape(1)
    gates = jnp.where(single, head_mask[:1], head_mask)
    attn_cat, log_total = attend(lone_flag, gates, queries, keys_all, values_all)
    branch = jnp.dot(attn_cat, full_proj, preferred_element_type=jnp.float32) + proj_bias.astype(
        jnp.float32
    )
    branch = branch.reshape(blocked)
    middle = tok_float + first_gate * branch
    second_normal, second_inv = norm_stats(middle)
    second_in = (second_normal * (1.0 + second_scale) + second_shift).astype(jnp.bfloat16)
    second_in = second_in.reshape(flat)

    grad_final = cotangent.astype(jnp.float32).reshape(blocked)
    grad_out = (keep_rows * second_gate * grad_final).astype(jnp.bfloat16).reshape(flat)
    down_bias_grad = jnp.sum(grad_out.astype(jnp.float32), axis=0)
    plan = sum_plan()
    core, across = plan[0], plan[1]
    mp_steps = len(levels_of("mp"))

    pre_act = jnp.dot(second_in, full_up, preferred_element_type=jnp.float32) + up_bias.astype(
        jnp.float32
    )
    value, slope = gelu_parts(pre_act.reshape(slot_count, slot_rows, hidden_width))
    hidden = (value * unit_gate).astype(jnp.bfloat16).reshape(row_count, hidden_width)

    down_sum = ready(grad_product(hidden, grad_out), core)
    hidden, down_sum = tie(hidden, down_sum)
    down_sum = launch(down_sum, core)
    mlp_out = (
        jnp.dot(hidden, full_down, preferred_element_type=jnp.float32)
        + down_bias.astype(jnp.float32)
    ).astype(jnp.bfloat16)
    mlp_float = mlp_out.astype(jnp.float32).reshape(blocked)
    output = (middle + keep_rows * second_gate * mlp_float).astype(jnp.bfloat16).reshape(flat)
    grad_second_gate = jnp.sum(keep_rows * grad_final * mlp_float, axis=1)

    down_sum = ready(settle(down_sum, core), across)
    grad_out, down_sum = tie(grad_out, down_sum)
    down_sum = launch(down_sum, across)
    grad_hidden = jnp.einsum(
        "nd,fd->nf", grad_out, full_down, preferred_element_type=jnp.float32
    ).reshape(slot_count, slot_rows, hidden_width)
    grad_pre = (grad_hidden * unit_gate * slope).astype(jnp.bfloat16)
    grad_pre = grad_pre.reshape(row_count, hidden_width)
    up_bias_grad = jnp.sum(grad_pre.astype(jnp.float32), axis=0)

    up_sum = ready(grad_product(second_in, grad_pre), core)
    grad_pre, up_sum = tie(grad_pre, up_sum)
    up_sum = launch(up_sum, core)
    grad_second = jnp.einsum("nf,df->nd", grad_pre, full_up, preferred_element_type=jnp.float32)
    grad_second = grad_second.astype(jnp.bfloat16)
    up_sum = ready(settle(up_sum, core), across)
    grad_second, up_sum = tie(grad_second, up_sum)
    up_sum = launch(up_sum, across)
    grad_second = grad_second.astype(jnp.float32).reshape(blocked)

    grad_second_scale = jnp.sum(grad_second * second_normal, axis=1)
    grad_second_shift = jnp.sum(grad_second, axis=1)
    grad_middle = grad_final + norm_back(
        grad_second * (1.0 + second_scale), second_inv, second_normal
    )
    grad_branch = (first_gate * grad_middle).astype(jnp.bfloat16).reshape(flat)
    grad_first_gate = jnp.sum(grad_middle * branch, axis=1)
    grad_cat = jnp.einsum(
        "ne,de->nd", grad_branch, full_proj, preferred_element_type=jnp.float32
    ).astype(jnp.bfloat16)
    proj_sum = ready(grad_product(attn_cat, grad_branch), core)
    proj_bias_grad = jnp.sum(grad_branch.astype(jnp.float32), axis=0)
    down_sum = ready(settle(down_sum, across), plan[2])
    grad_cat, proj_sum, down_sum = tie(grad_cat, proj_sum, down_sum)
    proj_sum = launch(proj_sum, core)
    down_sum = launch(down_sum, plan[2])

    attn_args = (lone_flag, gates, queries, keys_all, values_all)
    low_part = attend_back(*attn_args, grad_cat, log_total, 0, 2)
    low_width = low_part.shape[1] // 3
    low_done = low_width - LANES
    low_cols = jnp.concatenate(
        [low_part[:, part * low_width : part * low_width + low_done] for part in range(3)], axis=1
    )
    low_sum = ready(grad_product(normed, low_cols), core)
    down_sum = ready(settle(down_sum, plan[2]), plan[3])
    up_sum = ready(settle(up_sum, across), plan[2])
    proj_sum = ready(settle(proj_sum, core), across)
    low_part, low_sum, down_sum, up_sum, proj_sum = tie(
        low_part, low_sum, down_sum, up_sum, proj_sum
    )
    low_sum = launch(low_sum, core)
    proj_sum = launch(proj_sum, across)
    up_sum = launch(up_sum, plan[2])
    down_sum = launch(down_sum, plan[3])

    high_cols = attend_back(*attn_args, grad_cat, log_total, 1, 2, low_part)
    high_width = high_cols.shape[1] // 3
    low_sum = ready(settle(low_sum, core), across)
    high_cols, low_sum = tie(high_cols, low_sum)
    low_sum = launch(low_sum, across)
    high_sum = ready(grad_product(normed, high_cols), core)
    high_cols, high_sum = tie(high_cols, high_sum)
    up_sum = ready(settle(up_sum, plan[2]), plan[3])
    proj_sum = ready(settle(proj_sum, across), plan[2])
    down_sum = ready(settle(down_sum, plan[3]), plan[4])
    high_sum = launch(high_sum, core)

    def interleave(low, high):
        return jnp.concatenate(
            [
                piece
                for part in range(3)
                for piece in (
                    low[:, part * low_done : (part + 1) * low_done],
                    high[:, part * high_width : (part + 1) * high_width],
                )
            ],
            axis=1,
        )

    grad_joined = interleave(low_cols, high_cols)
    high_sum = ready(settle(high_sum, core), across)
    grad_joined, high_sum, up_sum, proj_sum, down_sum = tie(
        grad_joined, high_sum, up_sum, proj_sum, down_sum
    )
    high_sum = launch(high_sum, across)
    up_sum = launch(up_sum, plan[3])
    proj_sum = launch(proj_sum, plan[2])
    down_sum = launch(down_sum, plan[4])
    grad_normed = jnp.einsum("ne,de->nd", grad_joined, full_qkv, preferred_element_type=jnp.float32)
    column_sums = jnp.sum(grad_joined.astype(jnp.float32), axis=0)
    qv_bias_grad = jnp.concatenate([column_sums[:model_width], column_sums[2 * model_width :]])
    qkv_sum = interleave(settle(low_sum, across), settle(high_sum, across))
    qkv_sum = ready(qkv_sum, plan[2])
    grad_normed, qkv_sum = tie(grad_normed, qkv_sum)
    qkv_sum = launch(qkv_sum, plan[2])

    grad_normed = grad_normed.reshape(blocked)
    token_grad = grad_middle + norm_back(grad_normed * (1.0 + first_scale), first_inv, first_normal)
    grad_first_scale = jnp.sum(grad_normed * first_normal, axis=1)
    grad_first_shift = jnp.sum(grad_normed, axis=1)

    lone = jnp.arange(slot_count)[:, None] == 0
    sums = jnp.concatenate(
        [
            grad_first_shift,
            grad_first_scale,
            grad_first_gate,
            grad_second_shift,
            grad_second_scale,
            grad_second_gate,
        ],
        axis=1,
    )
    grad_modulation = jnp.where(
        single, jnp.where(lone, jnp.sum(sums, axis=0, keepdims=True), 0.0), sums
    )
    biases = jnp.concatenate(
        [
            jnp.sum(grad_modulation, axis=0),
            qv_bias_grad,
            proj_bias_grad,
            up_bias_grad,
            down_bias_grad,
        ]
    )
    mp_plan = plan[:mp_steps]
    near_plan = column_plan()
    biases = double_all(biases, jnp.add, mp_plan + near_plan)
    mod_cols = grad_modulation
    for step in near_plan:
        kept, sent = ready(mod_cols, step)
        other = swap(sent, step[1], 1 << step[2])
        mod_cols = join(pick(kept, step[0], step[3], my_bit(step)), other)
    mod_cols = double_all(mod_cols, join, mp_plan)
    all_stamps = double_all(stamp_float, join, near_plan + mp_plan)
    cond_cols = condition_of(all_stamps).astype(jnp.float32)
    ada_piece = jnp.einsum("sd,sc->dc", cond_cols, mod_cols, precision=HIGHEST)
    ends = [6 * model_width, 8 * model_width, 9 * model_width, 9 * model_width + hidden_width]
    return (
        output,
        token_grad.reshape(flat),
        ada_piece,
        finish(qkv_sum, plan[2:]),
        finish(proj_sum, plan[2:]),
        finish(up_sum, plan[3:]),
        finish(down_sum, plan[4:]),
        *jnp.split(biases, ends),
    )


def solution(mesh):
    in_specs = (
        P(("seq", "mp"), None),
        P(("seq", "mp"), None),
        P(("seq", "mp")),
        P(("seq", "mp")),
        P(("seq", "mp"), None),
        P(("seq", "mp"), None),
        P(("seq", "mp")),
        P("mp", None),
        P(),
        P("mp", None),
        P(),
        P("mp", None),
        P(),
        P("mp", None),
        P(),
        P("mp", None),
        P(),
    )
    out_specs = (
        P(("seq", "mp"), None),
        P(("seq", "mp"), None),
        P("mp", "seq"),
        P("mp", "seq"),
        P("mp", "seq"),
        P("mp", "seq"),
        P("mp", "seq"),
        P(),
        P(),
        P(),
        P(),
        P(),
    )

    return jax.shard_map(
        on_device, mesh=mesh, in_specs=in_specs, out_specs=out_specs, check_vma=False
    )
```
